32 devices in a mesh: band: 4 (over x, core), lev: 8 (over z, y).
Axes of the slice: x: 2, y: 2, z: 4, core: 2. Of those that a mesh axis runs over, the one named last changes fastest.
Arguments:
- grid_in: bfloat16 [3, 32, 16, 2688], P(None, 'lev', 'band'), may hold values from -6 to 6
- row_shift: int32 [16], P('band'), may hold values from -3 to 0
- block_shift: int32 [16], P('band'), may hold values from 0 to 20
- interp_weights: bfloat16 [16, 4, 3, 128, 128], P('band'), may hold values from -0.15625 to 0.15625
- wave_order: int32 [128], replicated, may hold values from 0 to 127, as said below
- legendre: bfloat16 [128, 16, 1280], P('band'), may hold values from -1.5 to 1.5
Outputs:
- spectral: bfloat16 [3, 32, 128, 2, 1280], P(None, 'lev', 'band')
The draws below stay inside these ranges and needn't reach their ends.
Inputs may be any that keep to these rules, and one draw needn't show every extreme that they name: `row_shift`: each latitude's stencil rows lie within 3 rows of it on both sides. `wave_order`: a permutation of the 128 wavenumbers; slots d * 32 to (d + 1) * 32 - 1 hold exactly one wavenumber of each aligned run of 4 consecutive wavenumbers.
All inputs are finite; a program needn't handle non-finite values.
Results may differ from the reference program's by a relative error of at most 0.0065.
Values may be sent and summed in bfloat16 or wider, within the bound.
A program may use at most 128 MiB of HBM per device.

```python
import math
import jax
import jax.numpy as jnp
from jax import lax

F = 3
M_DEV = 32
NN = 1280
BLK = 128
NBLK = 21
HALO = 3
STENCIL = 4
NLON = 2688
NLAT = 16
LEVELS = 32
NM = 128
N_BAND = 4


def draw_wave_order(key, part):
    bands = NM // M_DEV
    keys = jax.random.split(key, M_DEV)
    shuffled = jax.vmap(lambda single: jax.random.permutation(single, bands))(keys)
    base = jnp.arange(M_DEV, dtype=jnp.int32)[:, None] * bands
    owners = base + shuffled.astype(jnp.int32)
    return owners.T.reshape(NM).astype(jnp.int32)


def set_ends(drawn, own_key, low, high):
    extent = drawn.shape
    index_at = [jax.random.randint(jax.random.fold_in(own_key, axis), (), 0, extent[axis]) for axis in range(len(extent))]
    drawn = drawn.at[tuple(index_at)].set(low)
    longest = extent.index(max(extent))
    index_at[longest] = (index_at[longest] + 1) % extent[longest]
    return drawn.at[tuple(index_at)].set(high)


def steps_of(stream_key, shape, cuts, low, top_value):
    gain, own = 1.0, jax.random.fold_in(stream_key, 6)
    for position, blocks in cuts:
        draws = jnp.exp(jax.random.uniform(jax.random.fold_in(own, position), (blocks,), jnp.float32, low / len(cuts), top_value / len(cuts)))
        gain = gain * jnp.repeat(draws, shape[position] // blocks).reshape([-1 if axis == position else 1 for axis in range(len(shape))])
    return gain


def bell_draw(own_key, extent, deviation, most, cuts=(), kind=jnp.bfloat16):
    values = jax.random.normal(own_key, extent, jnp.float32) * deviation
    if len(cuts) > 0:
        values = steps_of(own_key, extent, cuts, -0.22, 0.18) * values
    return jnp.clip(values, min=-most, max=most).astype(kind)


def setup_inputs(seed: int = 0) -> dict:
    streams_of = jax.random.split(jax.random.key(seed), 7)
    return {
        "grid_in": bell_draw(streams_of[0], (F, LEVELS, NLAT, NLON), 1.0, 6.0, ((1, 8), (2, 4))),
        "row_shift": set_ends(jax.random.randint(streams_of[1], (NLAT,), 0 - HALO, HALO - STENCIL + 2), jax.random.fold_in(streams_of[1], 1), 0 - HALO, (HALO - STENCIL + 2) - 1).astype(jnp.int32),
        "block_shift": set_ends(jax.random.randint(streams_of[2], (NLAT,), 0, NBLK), jax.random.fold_in(streams_of[2], 1), 0, NBLK - 1).astype(jnp.int32),
        "interp_weights": bell_draw(streams_of[3], (NLAT, STENCIL, 3, BLK, BLK), (STENCIL * 3 * BLK) ** -0.5, 0.15625, ((0, 4),)),
        "wave_order": draw_wave_order(jax.random.fold_in(streams_of[6], 71), 0),
        "legendre": bell_draw(streams_of[5], (NM, NLAT, NN), NLAT ** -0.5, 1.5, ((0, 4),)),
    }


def make_table(waves, longitudes):
    column = jnp.arange(longitudes, dtype=jnp.int32)[:, None]
    phase = column * waves.astype(jnp.int32)[None, :] % longitudes
    angle = phase.astype(jnp.float32) * (2.0 * math.pi / longitudes)
    paired = jnp.stack([jnp.cos(angle), -jnp.sin(angle)], axis=2)
    return (paired.reshape(longitudes, 2 * waves.shape[0]) / math.sqrt(longitudes)).astype(jnp.bfloat16)

def reference(grid_in, row_shift, block_shift, interp_weights, wave_order, legendre):
    padded = jnp.pad(grid_in, ((0, 0), (1, 1), (HALO, HALO), (0, 0)))

    def one_row(inputs):
        row_index, weights = inputs
        start = (row_index + HALO + row_shift[row_index]).astype(jnp.int32)
        rows = lax.dynamic_slice_in_dim(padded, start, STENCIL, 2)
        rows = jnp.roll(rows, -block_shift[row_index] * BLK, axis=3)
        rows = rows.reshape(F, LEVELS + 2, STENCIL, NBLK, BLK)
        stacked = jnp.stack([rows[:, level_step:level_step + LEVELS] for level_step in range(3)], axis=3)
        result = jnp.einsum('flsvbj,svji->flbi', stacked.astype(jnp.float32), weights.astype(jnp.float32))
        return result.reshape(F, LEVELS, NLON)
    per_row = lax.map(one_row, (jnp.arange(NLAT, dtype=jnp.int32), interp_weights))
    interp = jnp.transpose(per_row, (1, 2, 0, 3)).astype(jnp.bfloat16)
    table = make_table(wave_order, NLON)
    fourier = jnp.dot(interp.reshape(F * LEVELS * NLAT, NLON), table, preferred_element_type=jnp.float32)
    fourier = fourier.astype(jnp.bfloat16).reshape(F * LEVELS, NLAT, N_BAND, M_DEV, 2)
    fourier = jnp.transpose(fourier, (2, 0, 1, 3, 4))
    degree = jnp.arange(NN, dtype=jnp.int32)[None, :]
    keep = (degree >= wave_order[:, None]).reshape(N_BAND, M_DEV, NN)
    blocks_all = legendre.reshape(N_BAND, M_DEV, NLAT, NN)

    def one_group(inputs):
        coeffs, blocks, kept = inputs
        result = jnp.einsum('arqc,qrn->aqcn', coeffs.astype(jnp.float32), blocks.astype(jnp.float32))
        result = jnp.where(kept[None, :, None, :], result, jnp.zeros((), jnp.float32))
        return result.astype(jnp.bfloat16)
    grouped = lax.map(one_group, (fourier, blocks_all, keep))
    spectral = jnp.transpose(grouped, (1, 0, 2, 3, 4)).reshape(F, LEVELS, NM, 2, NN)
    return spectral
```

```python
import functools
import math

import jax
import jax.numpy as jnp
from jax import lax
from jax.experimental import pallas as pl
from jax.experimental.pallas import tpu as pltpu
from jax.sharding import PartitionSpec as P

BLK = 128
HALO = 3
STENCIL = 4
MESH = pl.DeviceIdType.MESH
DIRECTIONS = [(db, dl) for db in (-1, 0, 1) for dl in (-1, 0, 1) if (db, dl) != (0, 0)]


def round_up(value, multiple):
    return -(-value // multiple) * multiple


def spectral_kernel(
    bands, levs, fields, x_ref, w_ref, row_ref, block_ref, wave_ref, out_ref,
    ext, table, picks, shifted, outgoing, incoming, halo_send, halo_recv, all_send, all_recv,
):
    band, lev = lax.axis_index("band"), lax.axis_index("lev")
    lat_rows, depth, packed, _ = x_ref.shape
    waves = wave_ref.shape[1]
    owned = waves // bands
    items = fields * depth
    slots = shifted.shape[2]
    blocks = shifted.shape[1]
    longitudes = blocks * BLK

    def exists(db, dl):
        ok = None
        for here, step, count in ((band, db, bands), (lev, dl, levs)):
            if step == 0:
                continue
            one = here + 1 < count if step > 0 else here > 0
            ok = one if ok is None else jnp.logical_and(ok, one)
        return ok

    barrier = pltpu.get_barrier_semaphore()
    for k in range(1, bands):
        pl.semaphore_signal(
            barrier, inc=1, device_id={"band": lax.rem(band + k, bands), "lev": lev},
            device_id_type=MESH,
        )
    for db, dl in DIRECTIONS:
        if dl != 0:
            @pl.when(exists(db, dl))
            def _(db=db, dl=dl):
                pl.semaphore_signal(
                    barrier, inc=1, device_id={"band": band + db, "lev": lev + dl},
                    device_id_type=MESH,
                )

    source_rows = {1: (lat_rows - HALO, HALO), -1: (0, HALO), 0: (0, lat_rows)}
    target_rows = {1: (0, HALO), -1: (HALO + lat_rows, HALO), 0: (HALO, lat_rows)}
    source_levels = {1: (depth - 1, 1), -1: (0, 1), 0: (0, depth)}
    target_levels = {1: (0, 1), -1: (depth + 1, 1), 0: (1, depth)}

    near_bands = 1 + jnp.minimum(band, 1) + jnp.minimum(bands - 1 - band, 1)
    near_levs = jnp.minimum(lev, 1) + jnp.minimum(levs - 1 - lev, 1)
    pl.semaphore_wait(barrier, bands - 1 + near_bands * near_levs)

    def halo_copy(n, db, dl):
        return pltpu.make_async_remote_copy(
            src_ref=x_ref.at[pl.ds(*source_rows[db]), pl.ds(*source_levels[dl])],
            dst_ref=ext.at[pl.ds(*target_rows[db]), pl.ds(*target_levels[dl])],
            send_sem=halo_send.at[n],
            recv_sem=halo_recv.at[n],
            device_id={"band": band + db, "lev": lev + dl},
            device_id_type=MESH,
        )

    for n, (db, dl) in enumerate(DIRECTIONS):
        @pl.when(exists(db, dl))
        def _(n=n, db=db, dl=dl):
            halo_copy(n, db, dl).start()

    for n, (db, dl) in enumerate(DIRECTIONS):
        @pl.when(jnp.logical_not(exists(-db, -dl)))
        def _(db=db, dl=dl):
            rows, levels = target_rows[db], target_levels[dl]
            ext[pl.ds(*rows), pl.ds(*levels)] = jnp.zeros(
                (rows[1], levels[1], packed, BLK), ext.dtype
            )
    ext[pl.ds(HALO, lat_rows), pl.ds(1, depth)] = x_ref[...]

    wave = wave_ref[...]
    unit = 2.0 * math.pi / longitudes
    inner = lax.broadcasted_iota(jnp.int32, (BLK, waves), 0) * wave
    inner = lax.rem(inner, longitudes).astype(jnp.float32) * unit
    norm = 1.0 / math.sqrt(longitudes)
    inner_cos, inner_sin = jnp.cos(inner) * norm, jnp.sin(inner) * norm
    outer_rows = round_up(blocks, 8)
    outer = lax.broadcasted_iota(jnp.int32, (outer_rows, waves), 0) * wave
    outer = lax.rem(outer, blocks).astype(jnp.float32) * (unit * BLK)
    outer_cos, outer_sin = jnp.cos(outer), jnp.sin(outer)
    for b in range(blocks):
        ca, sa = outer_cos[b : b + 1], outer_sin[b : b + 1]
        table[b * BLK : (b + 1) * BLK, :waves] = (ca * inner_cos - sa * inner_sin).astype(
            table.dtype
        )
        table[b * BLK : (b + 1) * BLK, waves:] = (-(sa * inner_cos + ca * inner_sin)).astype(
            table.dtype
        )

    span = depth * packed
    item = lax.broadcasted_iota(jnp.int32, (slots, span), 0)
    field = jnp.zeros_like(item)
    for f in range(1, fields):
        field = field + (item >= f * depth).astype(jnp.int32)
    base = (item - field * depth) * packed + field * blocks
    base = lax.broadcasted_iota(jnp.int32, (slots, span), 1) - base
    base = jnp.where(item < items, base, -1)
    for r in range(lat_rows):
        for b in range(blocks):
            moved = block_ref[r] + b
            moved = jnp.where(moved >= blocks, moved - blocks, moved)
            picks[r, b * slots : (b + 1) * slots] = (
                jnp.where(base == moved, 1.0, 0.0).astype(picks.dtype)
            )

    for n, (db, dl) in enumerate(DIRECTIONS):
        @pl.when(exists(-db, -dl))
        def _(n=n, db=db, dl=dl):
            halo_copy(n, db, dl).wait_recv()

    for r in range(lat_rows):
        start = r + HALO + row_ref[r]
        rows = [ext[start + s].reshape((depth + 2) * packed, BLK) for s in range(STENCIL)]
        weights = [
            jnp.concatenate([w_ref[r, s, v] for v in range(3)], axis=1) for s in range(STENCIL)
        ]
        both = jnp.dot(
            jnp.concatenate(rows, axis=1), jnp.concatenate(weights, axis=0),
            preferred_element_type=jnp.float32,
        )
        total = (
            both[:span, :BLK]
            + both[packed : packed + span, BLK : 2 * BLK]
            + both[2 * packed : 2 * packed + span, 2 * BLK :]
        )
        chosen = jnp.dot(
            picks[r], total.astype(jnp.bfloat16), preferred_element_type=jnp.float32
        )
        shifted[r] = chosen.astype(shifted.dtype).reshape(blocks, slots, BLK)

    stacked = jnp.concatenate(
        [shifted[:, b].reshape(lat_rows * slots, BLK) for b in range(blocks)], axis=1
    )
    fourier = jnp.dot(stacked, table[...], preferred_element_type=jnp.float32)
    lane = lax.broadcasted_iota(jnp.int32, (lat_rows * slots, BLK), 1)
    for d in range(bands):
        group, offset = d * owned // BLK * BLK, d * owned % BLK
        real = fourier[:, group : group + BLK]
        imag = fourier[:, waves + group : waves + group + BLK]
        real = pltpu.roll(real, (BLK - offset) % BLK, 1)
        imag = pltpu.roll(imag, (BLK + owned - offset) % BLK, 1)
        outgoing[d] = jnp.where(lane < owned, real, imag).astype(outgoing.dtype)

    def all_copy(k):
        target = lax.rem(band + k, bands)
        return pltpu.make_async_remote_copy(
            src_ref=outgoing.at[target],
            dst_ref=incoming.at[band],
            send_sem=all_send.at[k],
            recv_sem=all_recv.at[k],
            device_id={"band": target, "lev": lev},
            device_id_type=MESH,
        )

    for k in range(1, bands):
        all_copy(k).start()
    out_ref[band] = outgoing[band]
    for n, (db, dl) in enumerate(DIRECTIONS):
        @pl.when(exists(db, dl))
        def _(n=n, db=db, dl=dl):
            halo_copy(n, db, dl).wait_send()
    for k in range(1, bands):
        all_copy(k).wait_recv()
        origin = lax.rem(band + bands - k, bands)
        out_ref[origin] = incoming[origin]
    for k in range(1, bands):
        all_copy(k).wait_send()


def per_device(bands, levs, grid_in, row_shift, block_shift, interp_weights, wave_order, legendre):
    fields, depth, lat_rows, longitudes = grid_in.shape
    owned, latitudes, degrees = legendre.shape
    waves = wave_order.shape[0]
    blocks = longitudes // BLK
    items = fields * depth
    packed = round_up(fields * blocks, 16)
    slots = round_up(items, 16)
    x = grid_in.reshape(fields, depth, lat_rows, blocks, BLK)
    x = jnp.transpose(x, (2, 1, 0, 3, 4)).reshape(lat_rows, depth, fields * blocks, BLK)
    x = jnp.pad(x, ((0, 0), (0, 0), (0, packed - fields * blocks), (0, 0)))
    vmem, smem = pl.BlockSpec(memory_space=pltpu.VMEM), pl.BlockSpec(memory_space=pltpu.SMEM)
    bf16 = jnp.bfloat16
    coeffs = pl.pallas_call(
        functools.partial(spectral_kernel, bands, levs, fields),
        out_shape=jax.ShapeDtypeStruct((bands, lat_rows * slots, BLK), bf16),
        in_specs=[vmem, vmem, smem, smem, vmem],
        out_specs=vmem,
        scratch_shapes=[
            pltpu.VMEM((lat_rows + 2 * HALO, depth + 2, packed, BLK), bf16),
            pltpu.VMEM((longitudes, 2 * waves), bf16),
            pltpu.VMEM((lat_rows, blocks * slots, depth * packed), bf16),
            pltpu.VMEM((lat_rows, blocks, slots, BLK), bf16),
            pltpu.VMEM((bands, lat_rows * slots, BLK), bf16),
            pltpu.VMEM((bands, lat_rows * slots, BLK), bf16),
            pltpu.SemaphoreType.DMA((len(DIRECTIONS),)),
            pltpu.SemaphoreType.DMA((len(DIRECTIONS),)),
            pltpu.SemaphoreType.DMA((bands,)),
            pltpu.SemaphoreType.DMA((bands,)),
        ],
        compiler_params=pltpu.CompilerParams(
            collective_id=0, has_side_effects=True, vmem_limit_bytes=48 << 20
        ),
    )(x, interp_weights, row_shift, block_shift, wave_order.reshape(1, waves))
    shaped = coeffs.reshape(bands * lat_rows, slots, BLK)[:, :items, : 2 * owned]
    shaped = shaped.reshape(latitudes, items, 2, owned)
    own_waves = lax.dynamic_slice_in_dim(wave_order, lax.axis_index("band") * owned, owned)
    degree = jnp.arange(degrees, dtype=jnp.int32)[None, :]
    keep = degree >= own_waves[:, None]
    result = jnp.einsum("racq,qrn->aqcn", shaped, legendre, preferred_element_type=jnp.float32)
    result = jnp.where(keep[None, :, None, :], result, jnp.zeros((), jnp.float32))
    return result.astype(bf16).reshape(fields, depth, owned, 2, degrees)


def solution(mesh):
    return jax.shard_map(
        functools.partial(per_device, mesh.shape["band"], mesh.shape["lev"]),
        mesh=mesh,
        in_specs=(
            P(None, "lev", "band", None),
            P("band"),
            P("band"),
            P("band", None, None, None, None),
            P(),
            P("band", None, None),
        ),
        out_specs=P(None, "lev", "band", None, None),
        check_vma=False,
    )
```

```python
import functools
import math

import jax
import jax.numpy as jnp
from jax import lax
from jax.experimental import pallas as pl
from jax.experimental.pallas import tpu as pltpu
from jax.sharding import PartitionSpec as P

BLK = 128
HALO = 3
STENCIL = 4
MESH = pl.DeviceIdType.MESH
DIRECTIONS = [(db, dl) for db in (-1, 0, 1) for dl in (-1, 0, 1) if (db, dl) != (0, 0)]


def round_up(value, multiple):
    return -(-value // multiple) * multiple


def spectral_kernel(
    bands, levs, fields, x_ref, w_ref, row_ref, block_ref, wave_ref, out_ref,
    ext, table, picks, shifted, outgoing, incoming, halo_send, halo_recv, all_send, all_recv,
):
    band, lev = lax.axis_index("band"), lax.axis_index("lev")
    lat_rows, depth, packed, _ = x_ref.shape
    waves = wave_ref.shape[1]
    owned = waves // bands
    items = fields * depth
    slots = shifted.shape[2]
    blocks = shifted.shape[1]
    longitudes = blocks * BLK

    def exists(db, dl):
        ok = None
        for here, step, count in ((band, db, bands), (lev, dl, levs)):
            if step == 0:
                continue
            one = here + 1 < count if step > 0 else here > 0
            ok = one if ok is None else jnp.logical_and(ok, one)
        return ok

    barrier = pltpu.get_barrier_semaphore()
    for k in range(1, bands):
        pl.semaphore_signal(
            barrier, inc=1, device_id={"band": lax.rem(band + k, bands), "lev": lev},
            device_id_type=MESH,
        )
    for db, dl in DIRECTIONS:
        if dl != 0:
            @pl.when(exists(db, dl))
            def _(db=db, dl=dl):
                pl.semaphore_signal(
                    barrier, inc=1, device_id={"band": band + db, "lev": lev + dl},
                    device_id_type=MESH,
                )

    source_rows = {1: (lat_rows - HALO, HALO), -1: (0, HALO), 0: (0, lat_rows)}
    target_rows = {1: (0, HALO), -1: (HALO + lat_rows, HALO), 0: (HALO, lat_rows)}
    source_levels = {1: (depth - 1, 1), -1: (0, 1), 0: (0, depth)}
    target_levels = {1: (0, 1), -1: (depth + 1, 1), 0: (1, depth)}

    near_bands = 1 + jnp.minimum(band, 1) + jnp.minimum(bands - 1 - band, 1)
    near_levs = jnp.minimum(lev, 1) + jnp.minimum(levs - 1 - lev, 1)
    pl.semaphore_wait(barrier, bands - 1 + near_bands * near_levs)

    def halo_copy(n, db, dl):
        return pltpu.make_async_remote_copy(
            src_ref=x_ref.at[pl.ds(*source_rows[db]), pl.ds(*source_levels[dl])],
            dst_ref=ext.at[pl.ds(*target_rows[db]), pl.ds(*target_levels[dl])],
            send_sem=halo_send.at[n],
            recv_sem=halo_recv.at[n],
            device_id={"band": band + db, "lev": lev + dl},
            device_id_type=MESH,
        )

    for n, (db, dl) in enumerate(DIRECTIONS):
        @pl.when(exists(db, dl))
        def _(n=n, db=db, dl=dl):
            halo_copy(n, db, dl).start()

    for n, (db, dl) in enumerate(DIRECTIONS):
        @pl.when(jnp.logical_not(exists(-db, -dl)))
        def _(db=db, dl=dl):
            rows, levels = target_rows[db], target_levels[dl]
            ext[pl.ds(*rows), pl.ds(*levels)] = jnp.zeros(
                (rows[1], levels[1], packed, BLK), ext.dtype
            )
    ext[pl.ds(HALO, lat_rows), pl.ds(1, depth)] = x_ref[...]

    wave = wave_ref[...]
    unit = 2.0 * math.pi / longitudes
    inner = lax.broadcasted_iota(jnp.int32, (BLK, waves), 0) * wave
    inner = lax.rem(inner, longitudes).astype(jnp.float32) * unit
    norm = 1.0 / math.sqrt(longitudes)
    inner_cos, inner_sin = jnp.cos(inner) * norm, jnp.sin(inner) * norm
    outer_rows = round_up(blocks, 8)
    outer = lax.broadcasted_iota(jnp.int32, (outer_rows, waves), 0) * wave
    outer = lax.rem(outer, blocks).astype(jnp.float32) * (unit * BLK)
    outer_cos, outer_sin = jnp.cos(outer), jnp.sin(outer)
    for b in range(blocks):
        ca, sa = outer_cos[b : b + 1], outer_sin[b : b + 1]
        table[b * BLK : (b + 1) * BLK, :waves] = (ca * inner_cos - sa * inner_sin).astype(
            table.dtype
        )
        table[b * BLK : (b + 1) * BLK, waves:] = (-(sa * inner_cos + ca * inner_sin)).astype(
            table.dtype
        )

    span = depth * packed
    item = lax.broadcasted_iota(jnp.int32, (slots, span), 0)
    field = jnp.zeros_like(item)
    for f in range(1, fields):
        field = field + (item >= f * depth).astype(jnp.int32)
    base = (item - field * depth) * packed + field * blocks
    base = lax.broadcasted_iota(jnp.int32, (slots, span), 1) - base
    base = jnp.where(item < items, base, -1)
    for r in range(lat_rows):
        for b in range(blocks):
            moved = block_ref[r] + b
            moved = jnp.where(moved >= blocks, moved - blocks, moved)
            picks[r, b * slots : (b + 1) * slots] = (
                jnp.where(base == moved, 1.0, 0.0).astype(picks.dtype)
            )

    for n, (db, dl) in enumerate(DIRECTIONS):
        @pl.when(exists(-db, -dl))
        def _(n=n, db=db, dl=dl):
            halo_copy(n, db, dl).wait_recv()

    for r in range(lat_rows):
        start = r + HALO + row_ref[r]
        rows = [ext[start + s].reshape((depth + 2) * packed, BLK) for s in range(STENCIL)]
        weights = [
            jnp.concatenate([w_ref[r, s, v] for v in range(3)], axis=1) for s in range(STENCIL)
        ]
        both = jnp.dot(
            jnp.concatenate(rows, axis=1), jnp.concatenate(weights, axis=0),
            preferred_element_type=jnp.float32,
        )
        total = (
            both[:span, :BLK]
            + both[packed : packed + span, BLK : 2 * BLK]
            + both[2 * packed : 2 * packed + span, 2 * BLK :]
        )
        chosen = jnp.dot(
            picks[r], total.astype(jnp.bfloat16), preferred_element_type=jnp.float32
        )
        shifted[r] = chosen.astype(shifted.dtype).reshape(blocks, slots, BLK)

    stacked = jnp.concatenate(
        [shifted[:, b].reshape(lat_rows * slots, BLK) for b in range(blocks)], axis=1
    )
    fourier = jnp.dot(stacked, table[...], preferred_element_type=jnp.float32)
    lane = lax.broadcasted_iota(jnp.int32, (lat_rows * slots, BLK), 1)
    for d in range(bands):
        group, offset = d * owned // BLK * BLK, d * owned % BLK
        real = fourier[:, group : group + BLK]
        imag = fourier[:, waves + group : waves + group + BLK]
        real = pltpu.roll(real, (BLK - offset) % BLK, 1)
        imag = pltpu.roll(imag, (BLK + owned - offset) % BLK, 1)
        outgoing[d] = jnp.where(lane < owned, real, imag).astype(outgoing.dtype)

    def all_copy(k):
        target = lax.rem(band + k, bands)
        return pltpu.make_async_remote_copy(
            src_ref=outgoing.at[target],
            dst_ref=incoming.at[band],
            send_sem=all_send.at[k],
            recv_sem=all_recv.at[k],
            device_id={"band": target, "lev": lev},
            device_id_type=MESH,
        )

    for k in range(1, bands):
        all_copy(k).start()
    out_ref[band] = outgoing[band]
    for n, (db, dl) in enumerate(DIRECTIONS):
        @pl.when(exists(db, dl))
        def _(n=n, db=db, dl=dl):
            halo_copy(n, db, dl).wait_send()
    for k in range(1, bands):
        all_copy(k).wait_recv()
        origin = lax.rem(band + bands - k, bands)
        out_ref[origin] = incoming[origin]
    for k in range(1, bands):
        all_copy(k).wait_send()


def legendre_kernel(items, coeff_ref, legendre_ref, wave_ref, out_ref, spread, result, sems):
    owned, latitudes, degrees = legendre_ref.shape
    bands, rows, _ = coeff_ref.shape
    slots = bands * rows // latitudes
    group = BLK // latitudes
    high = 2 * group
    first = lax.axis_index("band") * owned

    row = lax.broadcasted_iota(jnp.int32, (BLK, BLK), 0)
    column = lax.broadcasted_iota(jnp.int32, (BLK, BLK), 1)
    swap = row == lax.div(column, 2) + lax.rem(column, 2) * owned
    swap = jnp.where(swap & (column < 2 * owned), 1.0, 0.0).astype(jnp.bfloat16)
    coeffs = coeff_ref[...].reshape(bands * rows, BLK)
    coeffs = jnp.dot(coeffs, swap, preferred_element_type=jnp.float32).astype(jnp.bfloat16)
    lane = lax.broadcasted_iota(jnp.int32, (bands * rows, BLK), 1)
    base = lax.broadcasted_iota(jnp.int32, (bands * rows, BLK), 0)
    base = base - lax.rem(lane, latitudes) * slots
    picks = [jnp.where(base == a, 1.0, 0.0).astype(jnp.bfloat16) for a in range(items)]
    wide = lax.dot_general(
        coeffs, jnp.concatenate(picks, axis=1), (((0,), (0,)), ((), ())),
        preferred_element_type=jnp.float32,
    )
    spread[...] = wide[: 2 * owned].astype(spread.dtype)

    row = lax.broadcasted_iota(jnp.int32, (high, BLK), 0)
    column = lax.broadcasted_iota(jnp.int32, (high, BLK), 1)
    diagonal = lax.div(row, 2) == lax.div(column, latitudes)
    diagonal = jnp.where(diagonal, 1.0, 0.0).astype(jnp.bfloat16)
    degree = lax.broadcasted_iota(jnp.int32, (latitudes, degrees), 1)
    width = 2 * BLK if degrees % (2 * BLK) == 0 else BLK

    def send(g):
        part = pl.ds(g * group, group)
        return pltpu.make_async_copy(result.at[:, part], out_ref.at[:, part], sems.at[g])

    for g in range(owned // group):
        left = jnp.concatenate(
            [
                spread[g * high : (g + 1) * high, a * BLK : (a + 1) * BLK] * diagonal
                for a in range(items)
            ],
            axis=0,
        )
        right = []
        for q in range(g * group, (g + 1) * group):
            tile = legendre_ref[q]
            right.append(jnp.where(degree >= wave_ref[first + q], tile, jnp.zeros_like(tile)))
        right = jnp.concatenate(right, axis=0)
        for n in range(0, degrees, width):
            total = jnp.dot(left, right[:, n : n + width], preferred_element_type=jnp.float32)
            result[:, g * group : (g + 1) * group, :, n : n + width] = total.astype(
                result.dtype
            ).reshape(items, group, 2, width)
        send(g).start()
    for g in range(owned // group):
        send(g).wait()


def legendre_tiled(coeffs, legendre, wave_order, items):
    owned, latitudes, degrees = legendre.shape
    shape = (items, owned, 2, degrees)
    vmem, smem = pl.BlockSpec(memory_space=pltpu.VMEM), pl.BlockSpec(memory_space=pltpu.SMEM)
    return pl.pallas_call(
        functools.partial(legendre_kernel, items),
        out_shape=jax.ShapeDtypeStruct(shape, jnp.bfloat16),
        in_specs=[vmem, vmem, smem],
        out_specs=pl.BlockSpec(memory_space=pltpu.HBM),
        scratch_shapes=[
            pltpu.VMEM((2 * owned, items * BLK), jnp.bfloat16),
            pltpu.VMEM(shape, jnp.bfloat16),
            pltpu.SemaphoreType.DMA((owned * latitudes // BLK,)),
        ],
        compiler_params=pltpu.CompilerParams(vmem_limit_bytes=16 << 20),
    )(coeffs, legendre, wave_order)


def legendre_einsum(coeffs, legendre, wave_order, items):
    owned, latitudes, degrees = legendre.shape
    shaped = coeffs.reshape(latitudes, -1, BLK)[:, :items, : 2 * owned]
    shaped = shaped.reshape(latitudes, items, 2, owned)
    own_waves = lax.dynamic_slice_in_dim(wave_order, lax.axis_index("band") * owned, owned)
    degree = jnp.arange(degrees, dtype=jnp.int32)[None, :]
    keep = degree >= own_waves[:, None]
    result = jnp.einsum("racq,qrn->aqcn", shaped, legendre, preferred_element_type=jnp.float32)
    result = jnp.where(keep[None, :, None, :], result, jnp.zeros((), jnp.float32))
    return result.astype(jnp.bfloat16)


def per_device(bands, levs, grid_in, row_shift, block_shift, interp_weights, wave_order, legendre):
    fields, depth, lat_rows, longitudes = grid_in.shape
    owned, latitudes, degrees = legendre.shape
    waves = wave_order.shape[0]
    blocks = longitudes // BLK
    items = fields * depth
    packed = round_up(fields * blocks, 16)
    slots = round_up(items, 16)
    x = grid_in.reshape(fields, depth, lat_rows, blocks, BLK)
    x = jnp.transpose(x, (2, 1, 0, 3, 4)).reshape(lat_rows, depth, fields * blocks, BLK)
    x = jnp.pad(x, ((0, 0), (0, 0), (0, packed - fields * blocks), (0, 0)))
    vmem, smem = pl.BlockSpec(memory_space=pltpu.VMEM), pl.BlockSpec(memory_space=pltpu.SMEM)
    bf16 = jnp.bfloat16
    coeffs = pl.pallas_call(
        functools.partial(spectral_kernel, bands, levs, fields),
        out_shape=jax.ShapeDtypeStruct((bands, lat_rows * slots, BLK), bf16),
        in_specs=[vmem, vmem, smem, smem, vmem],
        out_specs=vmem,
        scratch_shapes=[
            pltpu.VMEM((lat_rows + 2 * HALO, depth + 2, packed, BLK), bf16),
            pltpu.VMEM((longitudes, 2 * waves), bf16),
            pltpu.VMEM((lat_rows, blocks * slots, depth * packed), bf16),
            pltpu.VMEM((lat_rows, blocks, slots, BLK), bf16),
            pltpu.VMEM((bands, lat_rows * slots, BLK), bf16),
            pltpu.VMEM((bands, lat_rows * slots, BLK), bf16),
            pltpu.SemaphoreType.DMA((len(DIRECTIONS),)),
            pltpu.SemaphoreType.DMA((len(DIRECTIONS),)),
            pltpu.SemaphoreType.DMA((bands,)),
            pltpu.SemaphoreType.DMA((bands,)),
        ],
        compiler_params=pltpu.CompilerParams(
            collective_id=0, has_side_effects=True, vmem_limit_bytes=48 << 20
        ),
    )(x, interp_weights, row_shift, block_shift, wave_order.reshape(1, waves))
    fits = latitudes % 16 == 0 and BLK % latitudes == 0
    if fits and owned % (BLK // latitudes) == 0:
        spectral = legendre_tiled(coeffs, legendre, wave_order, items)
    else:
        spectral = legendre_einsum(coeffs, legendre, wave_order, items)
    return spectral.reshape(fields, depth, owned, 2, degrees)


def solution(mesh):
    return jax.shard_map(
        functools.partial(per_device, mesh.shape["band"], mesh.shape["lev"]),
        mesh=mesh,
        in_specs=(
            P(None, "lev", "band", None),
            P("band"),
            P("band"),
            P("band", None, None, None, None),
            P(),
            P("band", None, None),
        ),
        out_specs=P(None, "lev", "band", None, None),
        check_vma=False,
    )
```

```python
import functools
import math

import jax
import jax.numpy as jnp
from jax import lax
from jax.experimental import pallas as pl
from jax.experimental.pallas import tpu as pltpu
from jax.sharding import PartitionSpec as P

BLK = 128
HALO = 3
STENCIL = 4
MESH = pl.DeviceIdType.MESH
SIDES = (1, -1)


def round_up(value, multiple):
    return -(-value // multiple) * multiple


def spectral_kernel(
    bands, levs, fields, x_ref, w_ref, row_ref, block_ref, wave_ref, out_ref,
    ext, edges, table, picks, sums, shifted, outgoing, incoming,
    lev_send, lev_recv, band_send, band_recv, corner_send, corner_recv, all_send, all_recv,
):
    band, lev = lax.axis_index("band"), lax.axis_index("lev")
    lat_rows, depth, packed, _ = x_ref.shape
    waves = wave_ref.shape[1]
    owned = waves // bands
    items = fields * depth
    slots = shifted.shape[2]
    blocks = shifted.shape[1]
    longitudes = blocks * BLK

    def has(here, step, count):
        return here + 1 < count if step > 0 else here > 0

    barrier = pltpu.get_barrier_semaphore()
    for step in SIDES:
        @pl.when(has(lev, step, levs))
        def _(step=step):
            pl.semaphore_signal(
                barrier, inc=1, device_id={"band": band, "lev": lev + step}, device_id_type=MESH
            )
    for k in range(1, bands):
        pl.semaphore_signal(
            barrier, inc=1, device_id={"band": lax.rem(band + k, bands), "lev": lev},
            device_id_type=MESH,
        )

    first_row = {1: lat_rows - HALO, -1: 0}
    landing = {1: 0, -1: HALO + lat_rows}

    def lev_copy(n, step):
        return pltpu.make_async_remote_copy(
            src_ref=x_ref.at[:, depth - 1 if step > 0 else 0],
            dst_ref=edges.at[n, pl.ds(HALO, lat_rows)],
            send_sem=lev_send.at[n],
            recv_sem=lev_recv.at[n],
            device_id={"band": band, "lev": lev + step},
            device_id_type=MESH,
        )

    def band_copy(n, step):
        return pltpu.make_async_remote_copy(
            src_ref=x_ref.at[pl.ds(first_row[step], HALO)],
            dst_ref=ext.at[pl.ds(landing[step], HALO)],
            send_sem=band_send.at[n],
            recv_sem=band_recv.at[n],
            device_id={"band": band + step, "lev": lev},
            device_id_type=MESH,
        )

    def corner_copy(n, m, step):
        return pltpu.make_async_remote_copy(
            src_ref=edges.at[n, pl.ds(HALO + first_row[step], HALO)],
            dst_ref=edges.at[n, pl.ds(landing[step], HALO)],
            send_sem=corner_send.at[n, m],
            recv_sem=corner_recv.at[n, m],
            device_id={"band": band + step, "lev": lev},
            device_id_type=MESH,
        )

    near_levs = jnp.minimum(lev, 1) + jnp.minimum(levs - 1 - lev, 1)
    pl.semaphore_wait(barrier, bands - 1 + near_levs)
    for n, step in enumerate(SIDES):
        @pl.when(has(lev, step, levs))
        def _(n=n, step=step):
            lev_copy(n, step).start()
    for n, step in enumerate(SIDES):
        @pl.when(has(band, step, bands))
        def _(n=n, step=step):
            band_copy(n, step).start()

    for n, step in enumerate(SIDES):
        @pl.when(jnp.logical_not(has(band, -step, bands)))
        def _(step=step):
            ext[pl.ds(landing[step], HALO)] = jnp.zeros((HALO, depth, packed, BLK), ext.dtype)
            for m in range(2):
                edges[m, pl.ds(landing[step], HALO)] = jnp.zeros((HALO, packed, BLK), ext.dtype)

        @pl.when(jnp.logical_not(has(lev, -step, levs)))
        def _(n=n):
            edges[n] = jnp.zeros(edges.shape[1:], edges.dtype)
    ext[pl.ds(HALO, lat_rows)] = x_ref[...]

    wave = wave_ref[...]
    unit = 2.0 * math.pi / longitudes
    inner = lax.broadcasted_iota(jnp.int32, (BLK, waves), 0) * wave
    inner = lax.rem(inner, longitudes).astype(jnp.float32) * unit
    norm = 1.0 / math.sqrt(longitudes)
    inner_cos, inner_sin = jnp.cos(inner) * norm, jnp.sin(inner) * norm
    outer_rows = round_up(blocks, 8)
    outer = lax.broadcasted_iota(jnp.int32, (outer_rows, waves), 0) * wave
    outer = lax.rem(outer, blocks).astype(jnp.float32) * (unit * BLK)
    outer_cos, outer_sin = jnp.cos(outer), jnp.sin(outer)
    for b in range(blocks):
        ca, sa = outer_cos[b : b + 1], outer_sin[b : b + 1]
        table[b * BLK : (b + 1) * BLK, :waves] = (ca * inner_cos - sa * inner_sin).astype(
            table.dtype
        )
        table[b * BLK : (b + 1) * BLK, waves:] = (-(sa * inner_cos + ca * inner_sin)).astype(
            table.dtype
        )

    span = depth * packed
    item = lax.broadcasted_iota(jnp.int32, (slots, span), 0)
    field = jnp.zeros_like(item)
    for f in range(1, fields):
        field = field + (item >= f * depth).astype(jnp.int32)
    base = (item - field * depth) * packed + field * blocks
    base = lax.broadcasted_iota(jnp.int32, (slots, span), 1) - base
    base = jnp.where(item < items, base, -1)
    for r in range(lat_rows):
        for b in range(blocks):
            moved = block_ref[r] + b
            moved = jnp.where(moved >= blocks, moved - blocks, moved)
            picks[r, b * slots : (b + 1) * slots] = (
                jnp.where(base == moved, 1.0, 0.0).astype(picks.dtype)
            )

    for n, step in enumerate(SIDES):
        @pl.when(has(lev, -step, levs))
        def _(n=n, step=step):
            lev_copy(n, step).wait_recv()
            for m, side in enumerate(SIDES):
                @pl.when(has(band, side, bands))
                def _():
                    corner_copy(n, m, side).start()
    for n, step in enumerate(SIDES):
        @pl.when(has(band, -step, bands))
        def _(n=n, step=step):
            band_copy(n, step).wait_recv()

    def level(array, l, v):
        return array[l * packed : (l + 1) * packed, v * BLK : (v + 1) * BLK]

    for r in range(lat_rows):
        start = r + HALO + row_ref[r]
        rows = [ext[start + s].reshape(span, BLK) for s in range(STENCIL)]
        weights = [
            jnp.concatenate([w_ref[r, s, v] for v in range(3)], axis=1) for s in range(STENCIL)
        ]
        both = jnp.dot(
            jnp.concatenate(rows, axis=1), jnp.concatenate(weights, axis=0),
            preferred_element_type=jnp.float32,
        )
        for l in range(depth):
            total = level(both, l, 1)
            if l > 0:
                total = total + level(both, l - 1, 0)
            if l < depth - 1:
                total = total + level(both, l + 1, 2)
            sums[r, l] = total

    for n, step in enumerate(SIDES):
        for m, side in enumerate(SIDES):
            @pl.when(jnp.logical_and(has(lev, -step, levs), has(band, -side, bands)))
            def _(n=n, m=m, side=side):
                corner_copy(n, m, side).wait_recv()

    for r in range(lat_rows):
        start = r + HALO + row_ref[r]
        for n, v, l in ((0, 0, 0), (1, 2, depth - 1)):
            rows = [edges[n, start + s] for s in range(STENCIL)]
            weights = [w_ref[r, s, v] for s in range(STENCIL)]
            sums[r, l] += jnp.dot(
                jnp.concatenate(rows, axis=1), jnp.concatenate(weights, axis=0),
                preferred_element_type=jnp.float32,
            )
        total = sums[r].reshape(span, BLK).astype(jnp.bfloat16)
        chosen = jnp.dot(picks[r], total, preferred_element_type=jnp.float32)
        shifted[r] = chosen.astype(shifted.dtype).reshape(blocks, slots, BLK)

    stacked = jnp.concatenate(
        [shifted[:, b].reshape(lat_rows * slots, BLK) for b in range(blocks)], axis=1
    )
    fourier = jnp.dot(stacked, table[...], preferred_element_type=jnp.float32)
    lane = lax.broadcasted_iota(jnp.int32, (lat_rows * slots, BLK), 1)
    for d in range(bands):
        group, offset = d * owned // BLK * BLK, d * owned % BLK
        real = fourier[:, group : group + BLK]
        imag = fourier[:, waves + group : waves + group + BLK]
        real = pltpu.roll(real, (BLK - offset) % BLK, 1)
        imag = pltpu.roll(imag, (BLK + owned - offset) % BLK, 1)
        outgoing[d] = jnp.where(lane < owned, real, imag).astype(outgoing.dtype)

    def all_copy(k):
        target = lax.rem(band + k, bands)
        return pltpu.make_async_remote_copy(
            src_ref=outgoing.at[target],
            dst_ref=incoming.at[band],
            send_sem=all_send.at[k],
            recv_sem=all_recv.at[k],
            device_id={"band": target, "lev": lev},
            device_id_type=MESH,
        )

    for k in range(1, bands):
        all_copy(k).start()
    out_ref[band] = outgoing[band]
    for n, step in enumerate(SIDES):
        @pl.when(has(lev, step, levs))
        def _(n=n, step=step):
            lev_copy(n, step).wait_send()

        @pl.when(has(band, step, bands))
        def _(n=n, step=step):
            band_copy(n, step).wait_send()
            for m in range(2):
                @pl.when(has(lev, -SIDES[m], levs))
                def _():
                    corner_copy(m, n, step).wait_send()
    for k in range(1, bands):
        all_copy(k).wait_recv()
        origin = lax.rem(band + bands - k, bands)
        out_ref[origin] = incoming[origin]
    for k in range(1, bands):
        all_copy(k).wait_send()


def legendre_kernel(items, coeff_ref, legendre_ref, wave_ref, out_ref, spread, result, sems):
    owned, latitudes, degrees = legendre_ref.shape
    bands, rows, _ = coeff_ref.shape
    slots = bands * rows // latitudes
    group = BLK // latitudes
    high = 2 * group
    first = lax.axis_index("band") * owned

    row = lax.broadcasted_iota(jnp.int32, (BLK, BLK), 0)
    column = lax.broadcasted_iota(jnp.int32, (BLK, BLK), 1)
    swap = row == lax.div(column, 2) + lax.rem(column, 2) * owned
    swap = jnp.where(swap & (column < 2 * owned), 1.0, 0.0).astype(jnp.bfloat16)
    coeffs = coeff_ref[...].reshape(bands * rows, BLK)
    coeffs = jnp.dot(coeffs, swap, preferred_element_type=jnp.float32).astype(jnp.bfloat16)
    lane = lax.broadcasted_iota(jnp.int32, (bands * rows, BLK), 1)
    base = lax.broadcasted_iota(jnp.int32, (bands * rows, BLK), 0)
    base = base - lax.rem(lane, latitudes) * slots
    picks = [jnp.where(base == a, 1.0, 0.0).astype(jnp.bfloat16) for a in range(items)]
    wide = lax.dot_general(
        coeffs, jnp.concatenate(picks, axis=1), (((0,), (0,)), ((), ())),
        preferred_element_type=jnp.float32,
    )
    spread[...] = wide[: 2 * owned].astype(spread.dtype)

    row = lax.broadcasted_iota(jnp.int32, (high, BLK), 0)
    column = lax.broadcasted_iota(jnp.int32, (high, BLK), 1)
    diagonal = lax.div(row, 2) == lax.div(column, latitudes)
    diagonal = jnp.where(diagonal, 1.0, 0.0).astype(jnp.bfloat16)
    degree = lax.broadcasted_iota(jnp.int32, (latitudes, degrees), 1)
    width = 2 * BLK if degrees % (2 * BLK) == 0 else BLK

    def send(g):
        part = pl.ds(g * group, group)
        return pltpu.make_async_copy(result.at[:, part], out_ref.at[:, part], sems.at[g])

    for g in range(owned // group):
        left = jnp.concatenate(
            [
                spread[g * high : (g + 1) * high, a * BLK : (a + 1) * BLK] * diagonal
                for a in range(items)
            ],
            axis=0,
        )
        right = []
        for q in range(g * group, (g + 1) * group):
            tile = legendre_ref[q]
            right.append(jnp.where(degree >= wave_ref[first + q], tile, jnp.zeros_like(tile)))
        right = jnp.concatenate(right, axis=0)
        for n in range(0, degrees, width):
            total = jnp.dot(left, right[:, n : n + width], preferred_element_type=jnp.float32)
            result[:, g * group : (g + 1) * group, :, n : n + width] = total.astype(
                result.dtype
            ).reshape(items, group, 2, width)
        send(g).start()
    for g in range(owned // group):
        send(g).wait()


def legendre_tiled(coeffs, legendre, wave_order, items):
    owned, latitudes, degrees = legendre.shape
    shape = (items, owned, 2, degrees)
    vmem, smem = pl.BlockSpec(memory_space=pltpu.VMEM), pl.BlockSpec(memory_space=pltpu.SMEM)
    return pl.pallas_call(
        functools.partial(legendre_kernel, items),
        out_shape=jax.ShapeDtypeStruct(shape, jnp.bfloat16),
        in_specs=[vmem, vmem, smem],
        out_specs=pl.BlockSpec(memory_space=pltpu.HBM),
        scratch_shapes=[
            pltpu.VMEM((2 * owned, items * BLK), jnp.bfloat16),
            pltpu.VMEM(shape, jnp.bfloat16),
            pltpu.SemaphoreType.DMA((owned * latitudes // BLK,)),
        ],
        compiler_params=pltpu.CompilerParams(vmem_limit_bytes=16 << 20),
    )(coeffs, legendre, wave_order)


def legendre_einsum(coeffs, legendre, wave_order, items):
    owned, latitudes, degrees = legendre.shape
    shaped = coeffs.reshape(latitudes, -1, BLK)[:, :items, : 2 * owned]
    shaped = shaped.reshape(latitudes, items, 2, owned)
    own_waves = lax.dynamic_slice_in_dim(wave_order, lax.axis_index("band") * owned, owned)
    degree = jnp.arange(degrees, dtype=jnp.int32)[None, :]
    keep = degree >= own_waves[:, None]
    result = jnp.einsum("racq,qrn->aqcn", shaped, legendre, preferred_element_type=jnp.float32)
    result = jnp.where(keep[None, :, None, :], result, jnp.zeros((), jnp.float32))
    return result.astype(jnp.bfloat16)


def per_device(bands, levs, grid_in, row_shift, block_shift, interp_weights, wave_order, legendre):
    fields, depth, lat_rows, longitudes = grid_in.shape
    owned, latitudes, degrees = legendre.shape
    waves = wave_order.shape[0]
    blocks = longitudes // BLK
    items = fields * depth
    packed = round_up(fields * blocks, 16)
    slots = round_up(items, 16)
    x = grid_in.reshape(fields, depth, lat_rows, blocks, BLK)
    x = jnp.transpose(x, (2, 1, 0, 3, 4)).reshape(lat_rows, depth, fields * blocks, BLK)
    x = jnp.pad(x, ((0, 0), (0, 0), (0, packed - fields * blocks), (0, 0)))
    vmem, smem = pl.BlockSpec(memory_space=pltpu.VMEM), pl.BlockSpec(memory_space=pltpu.SMEM)
    bf16 = jnp.bfloat16
    coeffs = pl.pallas_call(
        functools.partial(spectral_kernel, bands, levs, fields),
        out_shape=jax.ShapeDtypeStruct((bands, lat_rows * slots, BLK), bf16),
        in_specs=[vmem, vmem, smem, smem, vmem],
        out_specs=vmem,
        scratch_shapes=[
            pltpu.VMEM((lat_rows + 2 * HALO, depth, packed, BLK), bf16),
            pltpu.VMEM((2, lat_rows + 2 * HALO, packed, BLK), bf16),
            pltpu.VMEM((longitudes, 2 * waves), bf16),
            pltpu.VMEM((lat_rows, blocks * slots, depth * packed), bf16),
            pltpu.VMEM((lat_rows, depth, packed, BLK), jnp.float32),
            pltpu.VMEM((lat_rows, blocks, slots, BLK), bf16),
            pltpu.VMEM((bands, lat_rows * slots, BLK), bf16),
            pltpu.VMEM((bands, lat_rows * slots, BLK), bf16),
            pltpu.SemaphoreType.DMA((2,)),
            pltpu.SemaphoreType.DMA((2,)),
            pltpu.SemaphoreType.DMA((2,)),
            pltpu.SemaphoreType.DMA((2,)),
            pltpu.SemaphoreType.DMA((2, 2)),
            pltpu.SemaphoreType.DMA((2, 2)),
            pltpu.SemaphoreType.DMA((bands,)),
            pltpu.SemaphoreType.DMA((bands,)),
        ],
        compiler_params=pltpu.CompilerParams(
            collective_id=0, has_side_effects=True, vmem_limit_bytes=48 << 20
        ),
    )(x, interp_weights, row_shift, block_shift, wave_order.reshape(1, waves))
    fits = latitudes % 16 == 0 and BLK % latitudes == 0
    if fits and owned % (BLK // latitudes) == 0:
        spectral = legendre_tiled(coeffs, legendre, wave_order, items)
    else:
        spectral = legendre_einsum(coeffs, legendre, wave_order, items)
    return spectral.reshape(fields, depth, owned, 2, degrees)


def solution(mesh):
    return jax.shard_map(
        functools.partial(per_device, mesh.shape["band"], mesh.shape["lev"]),
        mesh=mesh,
        in_specs=(
            P(None, "lev", "band", None),
            P("band"),
            P("band"),
            P("band", None, None, None, None),
            P(),
            P("band", None, None),
        ),
        out_specs=P(None, "lev", "band", None, None),
        check_vma=False,
    )
```

```python
import functools
import math

import jax
import jax.numpy as jnp
from jax import lax
from jax.experimental import pallas as pl
from jax.experimental.pallas import tpu as pltpu
from jax.sharding import PartitionSpec as P

BLK = 128
HALO = 3
STENCIL = 4
MESH = pl.DeviceIdType.MESH
SIDES = (1, -1)


def round_up(value, multiple):
    return -(-value // multiple) * multiple


def spectral_kernel(
    bands, levs, fields, x_ref, w_ref, row_ref, block_ref, wave_ref, out_ref,
    ext, edges, table, picks, sums, shifted, outgoing, incoming,
    lev_send, lev_recv, band_send, band_recv, corner_send, corner_recv, all_send, all_recv,
):
    band, lev = lax.axis_index("band"), lax.axis_index("lev")
    lat_rows, depth, packed, _ = x_ref.shape
    waves = wave_ref.shape[1]
    owned = waves // bands
    items = fields * depth
    slots = shifted.shape[2]
    blocks = shifted.shape[1]
    longitudes = blocks * BLK

    def has(here, step, count):
        return here + 1 < count if step > 0 else here > 0

    barrier = pltpu.get_barrier_semaphore()
    for step in SIDES:
        @pl.when(has(lev, step, levs))
        def _(step=step):
            pl.semaphore_signal(
                barrier, inc=1, device_id={"band": band, "lev": lev + step}, device_id_type=MESH
            )
    for k in range(1, bands):
        pl.semaphore_signal(
            barrier, inc=1, device_id={"band": lax.rem(band + k, bands), "lev": lev},
            device_id_type=MESH,
        )

    row_order = sorted(range(lat_rows), key=lambda i: -min(i, lat_rows - 1 - i))
    first_row = {1: lat_rows - HALO, -1: 0}
    landing = {1: 0, -1: HALO + lat_rows}

    def lev_copy(n, step, i):
        return pltpu.make_async_remote_copy(
            src_ref=x_ref.at[i, depth - 1 if step > 0 else 0],
            dst_ref=edges.at[n, HALO + i],
            send_sem=lev_send.at[n, i],
            recv_sem=lev_recv.at[n, i],
            device_id={"band": band, "lev": lev + step},
            device_id_type=MESH,
        )

    def band_copy(n, step):
        return pltpu.make_async_remote_copy(
            src_ref=x_ref.at[pl.ds(first_row[step], HALO)],
            dst_ref=ext.at[pl.ds(landing[step], HALO)],
            send_sem=band_send.at[n],
            recv_sem=band_recv.at[n],
            device_id={"band": band + step, "lev": lev},
            device_id_type=MESH,
        )

    def corner_copy(n, m, step, i):
        return pltpu.make_async_remote_copy(
            src_ref=edges.at[n, HALO + i],
            dst_ref=edges.at[n, landing[step] + i - first_row[step]],
            send_sem=corner_send.at[n, m, i],
            recv_sem=corner_recv.at[n, m, i],
            device_id={"band": band + step, "lev": lev},
            device_id_type=MESH,
        )

    def corner_rows(step):
        return range(first_row[step], first_row[step] + HALO)

    near_levs = jnp.minimum(lev, 1) + jnp.minimum(levs - 1 - lev, 1)
    pl.semaphore_wait(barrier, bands - 1 + near_levs)
    for n, step in enumerate(SIDES):
        @pl.when(has(lev, step, levs))
        def _(n=n, step=step):
            for i in row_order:
                lev_copy(n, step, i).start()
    for n, step in enumerate(SIDES):
        @pl.when(has(band, step, bands))
        def _(n=n, step=step):
            band_copy(n, step).start()

    for n, step in enumerate(SIDES):
        @pl.when(jnp.logical_not(has(band, -step, bands)))
        def _(step=step):
            ext[pl.ds(landing[step], HALO)] = jnp.zeros((HALO, depth, packed, BLK), ext.dtype)
            for m in range(2):
                edges[m, pl.ds(landing[step], HALO)] = jnp.zeros((HALO, packed, BLK), ext.dtype)

        @pl.when(jnp.logical_not(has(lev, -step, levs)))
        def _(n=n):
            edges[n] = jnp.zeros(edges.shape[1:], edges.dtype)
    ext[pl.ds(HALO, lat_rows)] = x_ref[...]

    wave = wave_ref[...]
    unit = 2.0 * math.pi / longitudes
    inner = lax.broadcasted_iota(jnp.int32, (BLK, waves), 0) * wave
    inner = lax.rem(inner, longitudes).astype(jnp.float32) * unit
    norm = 1.0 / math.sqrt(longitudes)
    inner_cos, inner_sin = jnp.cos(inner) * norm, jnp.sin(inner) * norm
    outer_rows = round_up(blocks, 8)
    outer = lax.broadcasted_iota(jnp.int32, (outer_rows, waves), 0) * wave
    outer = lax.rem(outer, blocks).astype(jnp.float32) * (unit * BLK)
    outer_cos, outer_sin = jnp.cos(outer), jnp.sin(outer)
    for b in range(blocks):
        ca, sa = outer_cos[b : b + 1], outer_sin[b : b + 1]
        table[b * BLK : (b + 1) * BLK, :waves] = (ca * inner_cos - sa * inner_sin).astype(
            table.dtype
        )
        table[b * BLK : (b + 1) * BLK, waves:] = (-(sa * inner_cos + ca * inner_sin)).astype(
            table.dtype
        )

    span = depth * packed
    item = lax.broadcasted_iota(jnp.int32, (slots, span), 0)
    field = jnp.zeros_like(item)
    for f in range(1, fields):
        field = field + (item >= f * depth).astype(jnp.int32)
    base = (item - field * depth) * packed + field * blocks
    base = lax.broadcasted_iota(jnp.int32, (slots, span), 1) - base
    base = jnp.where(item < items, base, -1)
    for r in range(lat_rows):
        for b in range(blocks):
            moved = block_ref[r] + b
            moved = jnp.where(moved >= blocks, moved - blocks, moved)
            picks[r, b * slots : (b + 1) * slots] = (
                jnp.where(base == moved, 1.0, 0.0).astype(picks.dtype)
            )

    for i in row_order:
        for n, step in enumerate(SIDES):
            @pl.when(has(lev, -step, levs))
            def _(i=i, n=n, step=step):
                lev_copy(n, step, i).wait_recv()
                for m, side in enumerate(SIDES):
                    if i in corner_rows(side):
                        @pl.when(has(band, side, bands))
                        def _():
                            corner_copy(n, m, side, i).start()
    for n, step in enumerate(SIDES):
        @pl.when(has(band, -step, bands))
        def _(n=n, step=step):
            band_copy(n, step).wait_recv()

    def level(array, l, v):
        return array[l * packed : (l + 1) * packed, v * BLK : (v + 1) * BLK]

    for r in range(lat_rows):
        start = r + HALO + row_ref[r]
        rows = [ext[start + s].reshape(span, BLK) for s in range(STENCIL)]
        weights = [
            jnp.concatenate([w_ref[r, s, v] for v in range(3)], axis=1) for s in range(STENCIL)
        ]
        both = jnp.dot(
            jnp.concatenate(rows, axis=1), jnp.concatenate(weights, axis=0),
            preferred_element_type=jnp.float32,
        )
        for l in range(depth):
            total = level(both, l, 1)
            if l > 0:
                total = total + level(both, l - 1, 0)
            if l < depth - 1:
                total = total + level(both, l + 1, 2)
            sums[r, l] = total

    for n, step in enumerate(SIDES):
        for m, side in enumerate(SIDES):
            @pl.when(jnp.logical_and(has(lev, -step, levs), has(band, -side, bands)))
            def _(n=n, m=m, side=side):
                for i in corner_rows(side):
                    corner_copy(n, m, side, i).wait_recv()

    for r in range(lat_rows):
        start = r + HALO + row_ref[r]
        for n, v, l in ((0, 0, 0), (1, 2, depth - 1)):
            rows = [edges[n, start + s] for s in range(STENCIL)]
            weights = [w_ref[r, s, v] for s in range(STENCIL)]
            sums[r, l] += jnp.dot(
                jnp.concatenate(rows, axis=1), jnp.concatenate(weights, axis=0),
                preferred_element_type=jnp.float32,
            )
        total = sums[r].reshape(span, BLK).astype(jnp.bfloat16)
        chosen = jnp.dot(picks[r], total, preferred_element_type=jnp.float32)
        shifted[r] = chosen.astype(shifted.dtype).reshape(blocks, slots, BLK)

    stacked = jnp.concatenate(
        [shifted[:, b].reshape(lat_rows * slots, BLK) for b in range(blocks)], axis=1
    )
    fourier = jnp.dot(stacked, table[...], preferred_element_type=jnp.float32)
    lane = lax.broadcasted_iota(jnp.int32, (lat_rows * slots, BLK), 1)
    for d in range(bands):
        group, offset = d * owned // BLK * BLK, d * owned % BLK
        real = fourier[:, group : group + BLK]
        imag = fourier[:, waves + group : waves + group + BLK]
        real = pltpu.roll(real, (BLK - offset) % BLK, 1)
        imag = pltpu.roll(imag, (BLK + owned - offset) % BLK, 1)
        outgoing[d] = jnp.where(lane < owned, real, imag).astype(outgoing.dtype)

    def all_copy(k):
        target = lax.rem(band + k, bands)
        return pltpu.make_async_remote_copy(
            src_ref=outgoing.at[target],
            dst_ref=incoming.at[band],
            send_sem=all_send.at[k],
            recv_sem=all_recv.at[k],
            device_id={"band": target, "lev": lev},
            device_id_type=MESH,
        )

    for k in range(1, bands):
        all_copy(k).start()
    out_ref[band] = outgoing[band]
    for n, step in enumerate(SIDES):
        @pl.when(has(lev, step, levs))
        def _(n=n, step=step):
            for i in range(lat_rows):
                lev_copy(n, step, i).wait_send()

        @pl.when(has(band, step, bands))
        def _(n=n, step=step):
            band_copy(n, step).wait_send()
            for m in range(2):
                @pl.when(has(lev, -SIDES[m], levs))
                def _():
                    for i in corner_rows(step):
                        corner_copy(m, n, step, i).wait_send()
    for k in range(1, bands):
        all_copy(k).wait_recv()
        origin = lax.rem(band + bands - k, bands)
        out_ref[origin] = incoming[origin]
    for k in range(1, bands):
        all_copy(k).wait_send()


def legendre_kernel(items, coeff_ref, legendre_ref, wave_ref, out_ref, spread, result, sems):
    owned, latitudes, degrees = legendre_ref.shape
    bands, rows, _ = coeff_ref.shape
    slots = bands * rows // latitudes
    group = BLK // latitudes
    high = 2 * group
    first = lax.axis_index("band") * owned

    row = lax.broadcasted_iota(jnp.int32, (BLK, BLK), 0)
    column = lax.broadcasted_iota(jnp.int32, (BLK, BLK), 1)
    swap = row == lax.div(column, 2) + lax.rem(column, 2) * owned
    swap = jnp.where(swap & (column < 2 * owned), 1.0, 0.0).astype(jnp.bfloat16)
    coeffs = coeff_ref[...].reshape(bands * rows, BLK)
    coeffs = jnp.dot(coeffs, swap, preferred_element_type=jnp.float32).astype(jnp.bfloat16)
    lane = lax.broadcasted_iota(jnp.int32, (bands * rows, BLK), 1)
    base = lax.broadcasted_iota(jnp.int32, (bands * rows, BLK), 0)
    base = base - lax.rem(lane, latitudes) * slots
    picks = [jnp.where(base == a, 1.0, 0.0).astype(jnp.bfloat16) for a in range(items)]
    wide = lax.dot_general(
        coeffs, jnp.concatenate(picks, axis=1), (((0,), (0,)), ((), ())),
        preferred_element_type=jnp.float32,
    )
    spread[...] = wide[: 2 * owned].astype(spread.dtype)

    row = lax.broadcasted_iota(jnp.int32, (high, BLK), 0)
    column = lax.broadcasted_iota(jnp.int32, (high, BLK), 1)
    diagonal = lax.div(row, 2) == lax.div(column, latitudes)
    diagonal = jnp.where(diagonal, 1.0, 0.0).astype(jnp.bfloat16)
    degree = lax.broadcasted_iota(jnp.int32, (latitudes, degrees), 1)
    width = 2 * BLK if degrees % (2 * BLK) == 0 else BLK

    def send(g):
        part = pl.ds(g * group, group)
        return pltpu.make_async_copy(result.at[:, part], out_ref.at[:, part], sems.at[g])

    for g in range(owned // group):
        left = jnp.concatenate(
            [
                spread[g * high : (g + 1) * high, a * BLK : (a + 1) * BLK] * diagonal
                for a in range(items)
            ],
            axis=0,
        )
        right = []
        for q in range(g * group, (g + 1) * group):
            tile = legendre_ref[q]
            right.append(jnp.where(degree >= wave_ref[first + q], tile, jnp.zeros_like(tile)))
        right = jnp.concatenate(right, axis=0)
        for n in range(0, degrees, width):
            total = jnp.dot(left, right[:, n : n + width], preferred_element_type=jnp.float32)
            result[:, g * group : (g + 1) * group, :, n : n + width] = total.astype(
                result.dtype
            ).reshape(items, group, 2, width)
        send(g).start()
    for g in range(owned // group):
        send(g).wait()


def legendre_tiled(coeffs, legendre, wave_order, items):
    owned, latitudes, degrees = legendre.shape
    shape = (items, owned, 2, degrees)
    vmem, smem = pl.BlockSpec(memory_space=pltpu.VMEM), pl.BlockSpec(memory_space=pltpu.SMEM)
    return pl.pallas_call(
        functools.partial(legendre_kernel, items),
        out_shape=jax.ShapeDtypeStruct(shape, jnp.bfloat16),
        in_specs=[vmem, vmem, smem],
        out_specs=pl.BlockSpec(memory_space=pltpu.HBM),
        scratch_shapes=[
            pltpu.VMEM((2 * owned, items * BLK), jnp.bfloat16),
            pltpu.VMEM(shape, jnp.bfloat16),
            pltpu.SemaphoreType.DMA((owned * latitudes // BLK,)),
        ],
        compiler_params=pltpu.CompilerParams(vmem_limit_bytes=16 << 20),
    )(coeffs, legendre, wave_order)


def legendre_einsum(coeffs, legendre, wave_order, items):
    owned, latitudes, degrees = legendre.shape
    shaped = coeffs.reshape(latitudes, -1, BLK)[:, :items, : 2 * owned]
    shaped = shaped.reshape(latitudes, items, 2, owned)
    own_waves = lax.dynamic_slice_in_dim(wave_order, lax.axis_index("band") * owned, owned)
    degree = jnp.arange(degrees, dtype=jnp.int32)[None, :]
    keep = degree >= own_waves[:, None]
    result = jnp.einsum("racq,qrn->aqcn", shaped, legendre, preferred_element_type=jnp.float32)
    result = jnp.where(keep[None, :, None, :], result, jnp.zeros((), jnp.float32))
    return result.astype(jnp.bfloat16)


def per_device(bands, levs, grid_in, row_shift, block_shift, interp_weights, wave_order, legendre):
    fields, depth, lat_rows, longitudes = grid_in.shape
    owned, latitudes, degrees = legendre.shape
    waves = wave_order.shape[0]
    blocks = longitudes // BLK
    items = fields * depth
    packed = round_up(fields * blocks, 16)
    slots = round_up(items, 16)
    x = grid_in.reshape(fields, depth, lat_rows, blocks, BLK)
    x = jnp.transpose(x, (2, 1, 0, 3, 4)).reshape(lat_rows, depth, fields * blocks, BLK)
    x = jnp.pad(x, ((0, 0), (0, 0), (0, packed - fields * blocks), (0, 0)))
    vmem, smem = pl.BlockSpec(memory_space=pltpu.VMEM), pl.BlockSpec(memory_space=pltpu.SMEM)
    bf16 = jnp.bfloat16
    coeffs = pl.pallas_call(
        functools.partial(spectral_kernel, bands, levs, fields),
        out_shape=jax.ShapeDtypeStruct((bands, lat_rows * slots, BLK), bf16),
        in_specs=[vmem, vmem, smem, smem, vmem],
        out_specs=vmem,
        scratch_shapes=[
            pltpu.VMEM((lat_rows + 2 * HALO, depth, packed, BLK), bf16),
            pltpu.VMEM((2, lat_rows + 2 * HALO, packed, BLK), bf16),
            pltpu.VMEM((longitudes, 2 * waves), bf16),
            pltpu.VMEM((lat_rows, blocks * slots, depth * packed), bf16),
            pltpu.VMEM((lat_rows, depth, packed, BLK), jnp.float32),
            pltpu.VMEM((lat_rows, blocks, slots, BLK), bf16),
            pltpu.VMEM((bands, lat_rows * slots, BLK), bf16),
            pltpu.VMEM((bands, lat_rows * slots, BLK), bf16),
            pltpu.SemaphoreType.DMA((2, lat_rows)),
            pltpu.SemaphoreType.DMA((2, lat_rows)),
            pltpu.SemaphoreType.DMA((2,)),
            pltpu.SemaphoreType.DMA((2,)),
            pltpu.SemaphoreType.DMA((2, 2, lat_rows)),
            pltpu.SemaphoreType.DMA((2, 2, lat_rows)),
            pltpu.SemaphoreType.DMA((bands,)),
            pltpu.SemaphoreType.DMA((bands,)),
        ],
        compiler_params=pltpu.CompilerParams(
            collective_id=0, has_side_effects=True, vmem_limit_bytes=48 << 20
        ),
    )(x, interp_weights, row_shift, block_shift, wave_order.reshape(1, waves))
    fits = latitudes % 16 == 0 and BLK % latitudes == 0
    if fits and owned % (BLK // latitudes) == 0:
        spectral = legendre_tiled(coeffs, legendre, wave_order, items)
    else:
        spectral = legendre_einsum(coeffs, legendre, wave_order, items)
    return spectral.reshape(fields, depth, owned, 2, degrees)


def solution(mesh):
    return jax.shard_map(
        functools.partial(per_device, mesh.shape["band"], mesh.shape["lev"]),
        mesh=mesh,
        in_specs=(
            P(None, "lev", "band", None),
            P("band"),
            P("band"),
            P("band", None, None, None, None),
            P(),
            P("band", None, None),
        ),
        out_specs=P(None, "lev", "band", None, None),
        check_vma=False,
    )
```
